32 devices in a mesh: groups: 2 (over x), blk: 16 (over z, y, core).
Axes of the slice: x: 2, y: 2, z: 4, core: 2. Of those that a mesh axis runs over, the one named last changes fastest.
Arguments:
- factors: bfloat16 [64, 2, 64, 128], P(('groups', 'blk')), parts along dimension 0, may hold values from -2.09375 to 2.09375
- token_mask: int32 [64, 64], P(('groups', 'blk')), parts along dimension 0, may hold values 0 or 1
- store: bfloat16 [16384, 2, 4096], P(('groups', 'blk')), parts along dimension 0, may hold values from -0.0625 to 0.0625
- inv_fisher: bfloat16 [2, 4096, 4096], P(None, 'blk'), as said below
- source_ids: int32 [16384], P(('groups', 'blk')), parts along dimension 0, may hold values from 0 to 15
- source_weight: float32 [16], replicated, may hold values from 0.25 to 4
Outputs:
- scores: float32 [64, 8192], P('groups', 'blk'), parts along dimension 0
The draws below stay inside these ranges and needn't reach their ends.
There are 2 independent parts, one for each index of `groups`. The reference program is written for one: setup_inputs(seed, part) draws one part's arguments, and reference() takes and returns one part's arrays. A program takes and returns all parts, laid end to end along the dimension named above; an argument that names none is the same for every part. Nothing has to cross between parts.
Inputs may be any that keep to these rules, and one draw needn't show every extreme that they name: `inv_fisher`: each layer's matrix is symmetric.
All inputs are finite; a program needn't handle non-finite values. No bound on the sum of `token_mask` on one device may be relied on, other than what follows from the above.
Results may differ from the reference program's by a relative error of at most 0.004.
Values may be sent and summed in bfloat16 or wider, within the bound.
A program may use at most 64 MiB of HBM per device.

```python
import math
import jax
import jax.numpy as jnp
from jax import lax

RANK = 64
FEAT = 4096
LAYERS = 2
SEQ = 64
NSRC = 16
N_DEV = 512
QUERIES = 32
TRAIN = 8192
N_BLK = 16


def draw_inv_fisher(key, part):
    diag_key = jax.random.fold_in(key, 11)
    off_key = jax.random.fold_in(key, 12)
    diagonal = jax.random.uniform(diag_key, (LAYERS, FEAT), jnp.float32, 1.0, 2.0)
    spread = 0.4
    gaussian = jax.random.normal(off_key, (LAYERS, FEAT, FEAT), jnp.float32)
    symmetric = (gaussian + jnp.swapaxes(gaussian, 1, 2)) * (spread / math.sqrt(2.0 * FEAT))
    identity = jnp.eye(FEAT, dtype=jnp.float32)
    return (symmetric + diagonal[:, :, None] * identity[None]).astype(jnp.bfloat16)


def set_ends(drawn, key, smallest, top_value):
    dims = drawn.shape
    index_at = [jax.random.randint(jax.random.fold_in(key, axis), (), 0, dims[axis]) for axis in range(len(dims))]
    drawn = drawn.at[tuple(index_at)].set(smallest)
    longest = dims.index(max(dims))
    index_at[longest] = (index_at[longest] + 1) % dims[longest]
    return drawn.at[tuple(index_at)].set(top_value)


def shard_levels(rng, shape, cuts, least, high):
    def one(position, parts):
        heights = jax.random.uniform(jax.random.fold_in(jax.random.fold_in(rng, 6), position), (parts,), jnp.float32, least / len(cuts), high / len(cuts))
        return jnp.repeat(jnp.exp(heights), shape[position] // parts).reshape((-1,) + (1,) * (len(shape) - position - 1))

    factor_of = one(*cuts[0])
    for cut in cuts[1:]:
        factor_of = factor_of * one(*cut)
    return factor_of


def noise(stream_key, shape, width, limit, shards=(), held_as=jnp.bfloat16):
    result = width * jax.random.normal(stream_key, shape, jnp.float32)
    if shards:
        result = result * shard_levels(stream_key, shape, shards, -0.22, 0.18)
    return jnp.clip(result, -limit, limit).astype(held_as)


def setup_inputs(seed: int = 0, part: int = 0) -> dict:
    streams_of = jax.random.split(jax.random.key(seed), 7)
    part_splits = jax.random.split(jax.random.fold_in(streams_of[6], part), 7)
    return {
        "factors": noise(part_splits[0], (QUERIES, LAYERS, SEQ, 2 * RANK), 0.35, 2.09375, ((0, 16),)),
        "token_mask": set_ends((jax.random.randint(part_splits[1], (QUERIES, SEQ), 0, 4) < 3).astype(jnp.int32), jax.random.fold_in(part_splits[1], 1), 0, 1),
        "store": noise(part_splits[2], (TRAIN, LAYERS, FEAT), (LAYERS * FEAT) ** -0.5, 0.0625, ((0, 16),)),
        "inv_fisher": draw_inv_fisher(jax.random.fold_in(streams_of[6], 71), part),
        "source_ids": set_ends(jax.random.randint(part_splits[4], (TRAIN,), 0, NSRC), jax.random.fold_in(part_splits[4], 1), 0, NSRC - 1).astype(jnp.int32),
        "source_weight": jnp.clip(jnp.exp(jax.random.uniform(streams_of[5], (NSRC,), jnp.float32, math.log(0.25), math.log(4.0))), 0.25, 4.0),
    }


def reference(factors, token_mask, store, inv_fisher, source_ids, source_weight):
    rank_size = factors.shape[3] // 2
    mask_values = token_mask.astype(jnp.float32)[:, None, :, None]
    left_side = factors[..., :rank_size].astype(jnp.float32) * mask_values
    right_side = factors[..., rank_size:].astype(jnp.float32)
    outer_sum = jnp.einsum("qlta,qltb->qlab", left_side, right_side)
    query_grads = outer_sum.reshape(outer_sum.shape[0], outer_sum.shape[1], rank_size * rank_size).astype(jnp.bfloat16)
    hidden = jnp.stack([jnp.dot(query_grads[:, layer_idx], inv_fisher[layer_idx], preferred_element_type=jnp.float32) for layer_idx in range(LAYERS)], axis=1).astype(jnp.bfloat16)
    flattened = hidden.reshape(hidden.shape[0], -1)
    blocks = store.reshape(N_BLK, N_DEV, -1)

    def score_block(block_rows):
        return jnp.dot(flattened, block_rows.T, preferred_element_type=jnp.float32)

    raw_scores = lax.map(score_block, blocks)
    raw_scores = jnp.transpose(raw_scores, (1, 0, 2)).reshape(flattened.shape[0], -1)
    scaling = source_weight[source_ids]
    return raw_scores * scaling[None, :]
```

```python
import functools
import jax
import jax.numpy as jnp
from jax import lax
from jax.experimental import pallas as pl
from jax.experimental.pallas import tpu as pltpu
from jax.sharding import PartitionSpec as P

LANES = 128
NT = (((1,), (1,)), ((), ()))


def make_grads(factors, token_mask):
    rank_size = factors.shape[3] // 2
    mask_values = token_mask.astype(jnp.float32)[:, None, :, None]
    left_side = factors[..., :rank_size].astype(jnp.float32) * mask_values
    right_side = factors[..., rank_size:].astype(jnp.float32)
    outer_sum = jnp.einsum("qlta,qltb->qlab", left_side, right_side)
    return outer_sum.reshape(outer_sum.shape[0], outer_sum.shape[1], rank_size * rank_size).astype(
        jnp.bfloat16
    )


def scale_of(source_ids, source_weight):
    matches = (
        source_ids[:, None] == jnp.arange(source_weight.shape[0], dtype=jnp.int32)[None, :]
    ).astype(jnp.float32)
    return jnp.sum(matches * source_weight[None, :], axis=1)


def plain(factors, token_mask, store, inv_fisher, source_ids, source_weight):
    query_grads = make_grads(factors, token_mask)
    layer_count = inv_fisher.shape[0]
    segment = lax.all_gather(query_grads, "blk", axis=0, tiled=True)
    products = [
        lax.dot_general(
            segment[:, layer_idx], inv_fisher[layer_idx], NT, preferred_element_type=jnp.float32
        )
        for layer_idx in range(layer_count)
    ]
    hidden_cols = jnp.stack(products, axis=1).astype(jnp.bfloat16)
    hidden = lax.all_to_all(hidden_cols, "blk", split_axis=0, concat_axis=2, tiled=True)
    raw_scores = lax.dot_general(
        lax.all_gather(hidden, "blk", axis=0, tiled=True),
        store,
        (((1, 2), (1, 2)), ((), ())),
        preferred_element_type=jnp.float32,
    )
    return raw_scores * scale_of(source_ids, source_weight)[None, :]


class Gather:
    def __init__(self, buf, send_sems, recv_sems, sizes):
        self.buf, self.send_sems, self.recv_sems = buf, send_sems, recv_sems
        self.outer, self.ys, self.cores = sizes
        me = lax.axis_index("blk")
        self.me = me
        self.c = lax.rem(me, self.cores)
        self.y = lax.rem(me // self.cores, self.ys)
        self.z = me // (self.cores * self.ys)
        self.sent = []

    def index(self, dz, dy, dc):
        if self.outer & (self.outer - 1):
            z = lax.rem(self.z + dz, self.outer)
        else:
            z, bit = self.z, 1
            while bit <= dz:
                if dz & bit:
                    z = z + bit - 2 * bit * lax.rem(z // bit, 2)
                bit *= 2
        y = lax.rem(self.y + dy, self.ys)
        c = lax.rem(self.c + dc, self.cores)
        return (z * self.ys + y) * self.cores + c

    def copy(self, slot, target, count):
        return pltpu.make_async_remote_copy(
            src_ref=self.buf.at[slot],
            dst_ref=self.buf.at[slot],
            send_sem=self.send_sems.at[count],
            recv_sem=self.recv_sems.at[slot],
            device_id={"blk": target},
            device_id_type=pl.DeviceIdType.MESH,
        )

    def send(self, slot, target):
        one = self.copy(slot, target, len(self.sent))
        one.start()
        self.sent.append(one)

    def arrive(self, slot):
        self.copy(slot, self.me, 0).wait_recv()

    def z_peers(self):
        return [self.index(k, 0, 0) for k in range(self.outer - 1, 0, -1)]

    def y_peers(self):
        return [self.index(0, k, 0) for k in range(1, self.ys)]

    def c_peers(self):
        return [self.index(0, 0, k) for k in range(1, self.cores)]

    def peers(self):
        return self.z_peers() + self.y_peers() + self.c_peers()

    def start(self):
        for target in self.z_peers() + self.y_peers() + self.c_peers():
            self.send(self.me, target)

    def z_slots(self):
        return [self.index(k, 0, 0) for k in range(1, self.outer)]

    def y_slots(self):
        return [self.index(k, j, 0) for k in range(self.outer) for j in range(1, self.ys)]

    def c_slots(self, near):
        return [
            self.index(k, j, i)
            for i in range(1, self.cores)
            for j in range(self.ys)
            for k in range(self.outer)
            if (j == 0) == near
        ]

    def take_z(self, slot):
        self.arrive(slot)
        for target in self.y_peers() + self.c_peers():
            self.send(slot, target)

    def take_y(self, slot):
        self.arrive(slot)
        for target in self.c_peers():
            self.send(slot, target)

    def finish(self):
        for one in self.sent:
            one.wait_send()


def kernel(
    sizes, mask_hbm, factors_hbm, ids_hbm, weight_hbm, fisher_hbm, store_hbm, out_ref,
    mask_ref, factors_ref, ids_ref, weight_ref,
    fisher, store, grads, hidden, spread, lhs, total, turned,
    send_sems, recv_sems, input_sems, fisher_sems, store_sem,
):
    nq, layers, _, width = factors_ref.shape
    rank = width // 2
    rows = rank * rank // LANES
    n = grads.shape[1]
    m = n * nq
    train = out_ref.shape[1]

    gathers = [
        [
            Gather(buf.at[l], send_sems.at[p, l], recv_sems.at[p, l], sizes)
            for l in range(layers)
        ]
        for p, buf in enumerate((grads, hidden))
    ]
    first = gathers[0][0]
    me = first.me
    barrier = pltpu.get_barrier_semaphore()
    peers = first.peers()
    for peer in peers:
        pl.semaphore_signal(
            barrier, inc=1, device_id={"blk": peer}, device_id_type=pl.DeviceIdType.MESH
        )
    inputs = [
        pltpu.make_async_copy(source, target, input_sems.at[i])
        for i, (source, target) in enumerate(
            (
                (factors_hbm, factors_ref),
                (mask_hbm, mask_ref),
                (ids_hbm, ids_ref),
                (weight_hbm, weight_ref),
            )
        )
    ]
    for one in inputs:
        one.start()
    fisher_copies = [
        pltpu.make_async_copy(fisher_hbm.at[l], fisher.at[l], fisher_sems.at[l])
        for l in range(layers)
    ]
    for one in fisher_copies:
        one.start()
    cols = store.shape[2]
    pairs = store_hbm.reshape(train * layers, store_hbm.shape[2])
    for slot in range(n):
        pltpu.make_async_copy(
            pairs.at[:, slot * cols : (slot + 1) * cols], store.at[slot], store_sem
        ).start()

    for one in inputs[:2]:
        one.wait()
    row = lax.broadcasted_iota(jnp.int32, (rows, width), 0)
    lane = lax.broadcasted_iota(jnp.int32, (rows, width), 1)
    picks = [(lane == 2 * row + par).astype(jnp.bfloat16) for par in range(2)]
    for l in range(layers):
        for q in range(nq):
            block = factors_ref[q, l]
            wide = block.astype(jnp.float32)
            high = lax.broadcasted_iota(jnp.int32, wide.shape, 1) >= rank
            rights = [
                jnp.where(high, 0.0, pltpu.roll(wide, rank, 1)).astype(jnp.bfloat16),
                jnp.where(high, wide, 0.0).astype(jnp.bfloat16),
            ]
            keep = mask_ref[q : q + 1, :].astype(jnp.float32)
            grad = None
            for par in range(2):
                left = lax.dot_general(picks[par], block, NT, preferred_element_type=jnp.float32)
                left = (left * keep).astype(jnp.bfloat16)
                term = jnp.dot(left, rights[par], preferred_element_type=jnp.float32)
                grad = term if grad is None else grad + term
            grads[l, me, q * rows : (q + 1) * rows, :] = grad.astype(jnp.bfloat16)
        if l == 0:
            pl.semaphore_wait(barrier, len(peers))
        gathers[0][l].start()
    for one in inputs[2:]:
        one.wait()
    ids = ids_ref[...]
    scale = jnp.zeros(ids.shape, jnp.float32)
    for source in range(weight_ref.shape[0]):
        scale = scale + jnp.where(ids == source, weight_ref[source], 0.0)

    def place(l, slot):
        for q in range(nq):
            spread[l, pl.ds(slot * nq + q, rows, stride=m), :] = grads[
                l, slot, q * rows : (q + 1) * rows, :
            ].astype(jnp.float32)

    for l in range(layers):
        place(l, me)
    for l in range(layers):
        one = gathers[0][l]
        for slot in one.z_slots():
            one.take_z(slot)
            place(l, slot)
    for l in range(layers):
        one = gathers[0][l]
        for slot in one.y_slots():
            one.take_y(slot)
            place(l, slot)
    for l in range(layers):
        one = gathers[0][l]
        for slot in one.c_slots(True):
            one.arrive(slot)
            place(l, slot)

    for l in range(layers):
        for slot in gathers[0][l].c_slots(False):
            gathers[0][l].arrive(slot)
            place(l, slot)
        for r in range(rows):
            lhs[:, r * LANES : (r + 1) * LANES] = spread[l, r * m : (r + 1) * m, :].astype(
                jnp.bfloat16
            )
        fisher_copies[l].wait()
        product = lax.dot_general(lhs[...], fisher[l], NT, preferred_element_type=jnp.float32)
        hidden[l, me] = product.astype(jnp.bfloat16)
        gathers[1][l].start()

    pltpu.make_async_copy(store, store, store_sem).wait()

    def add(slot, fresh=False):
        left = jnp.concatenate([hidden[l, slot] for l in range(layers)], axis=0)
        term = lax.dot_general(left, store[slot], NT, preferred_element_type=jnp.float32)
        total[...] = term if fresh else total[...] + term

    add(me, True)
    pair = gathers[1]
    slots = pair[0].z_slots()
    for one in pair[:-1]:
        for slot in slots:
            one.take_z(slot)
    for slot in slots:
        pair[-1].take_z(slot)
        add(slot)
    early = pair[0].c_slots(True)
    slots = pair[0].y_slots()
    for at in range(max(len(slots), len(early))):
        for slot in slots[at : at + 1]:
            for one in pair:
                one.take_y(slot)
            add(slot)
        for slot in early[at : at + 1]:
            for one in pair:
                one.arrive(slot)
            add(slot)
    for slot in pair[0].c_slots(False):
        for one in pair:
            one.arrive(slot)
        add(slot)

    turned[:, : layers * m] = total[...].T
    answer = None
    for l in range(layers):
        part = turned[pl.ds(l, train, stride=layers), :][:, l * m : (l + 1) * m]
        answer = part if answer is None else answer + part
    out_ref[...] = answer.T * scale
    for some in gathers:
        for one in some:
            one.finish()


def fused(n, factors, token_mask, store, inv_fisher, source_ids, source_weight):
    nq, layers, _, width = factors.shape
    train, _, feat = store.shape
    cols = inv_fisher.shape[1]
    m = n * nq
    rows = feat // LANES
    cores = 2 if n % 2 == 0 else 1
    ys = 2 if n % 4 == 0 else 1
    sizes = (n // (cores * ys), ys, cores)
    anyspace = pl.BlockSpec(memory_space=pl.ANY)
    return pl.pallas_call(
        functools.partial(kernel, sizes),
        out_shape=pltpu.VMEM((m, train), jnp.float32),
        in_specs=[anyspace] * 6,
        out_specs=pl.BlockSpec(memory_space=pltpu.VMEM),
        scratch_shapes=[
            pltpu.VMEM(token_mask.shape, token_mask.dtype),
            pltpu.VMEM(factors.shape, factors.dtype),
            pltpu.VMEM((1, train), source_ids.dtype),
            pltpu.SMEM(source_weight.shape, source_weight.dtype),
            pltpu.VMEM((layers, cols, feat), jnp.bfloat16),
            pltpu.VMEM((n, train * layers, cols), jnp.bfloat16),
            pltpu.VMEM((layers, n, nq * rows, LANES), jnp.bfloat16),
            pltpu.VMEM((layers, n, m, cols), jnp.bfloat16),
            pltpu.VMEM((layers, rows * m, LANES), jnp.float32),
            pltpu.VMEM((m, feat), jnp.bfloat16),
            pltpu.VMEM((layers * m, train * layers), jnp.float32),
            pltpu.VMEM((train * layers, LANES), jnp.float32),
            pltpu.SemaphoreType.DMA((2, layers, n)),
            pltpu.SemaphoreType.DMA((2, layers, n)),
            pltpu.SemaphoreType.DMA((4,)),
            pltpu.SemaphoreType.DMA((layers,)),
            pltpu.SemaphoreType.DMA(()),
        ],
        compiler_params=pltpu.CompilerParams(
            collective_id=0, has_side_effects=True, vmem_limit_bytes=60 * 2**20
        ),
        name="scores",
    )(token_mask, factors, source_ids[None, :], source_weight, inv_fisher, store)


def local(n, factors, token_mask, store, inv_fisher, source_ids, source_weight):
    nq, layers, _, width = factors.shape
    train, _, feat = store.shape
    cols = inv_fisher.shape[1]
    m = n * nq
    held = 2 * (inv_fisher.size + store.size) + 4 * layers * m * train * layers
    fits = (
        width == LANES
        and feat * 4 == width * width
        and cols % LANES == 0
        and layers == 2
        and m % 16 == 0
        and layers * m <= LANES
        and train % LANES == 0
        and held < 40 * 2**20
    )
    if not fits:
        return plain(factors, token_mask, store, inv_fisher, source_ids, source_weight)
    return fused(n, factors, token_mask, store, inv_fisher, source_ids, source_weight)


def solution(mesh):
    placed = (
        P(("groups", "blk"), None, None, None),
        P(("groups", "blk"), None),
        P(("groups", "blk"), None, None),
        P(None, "blk", None),
        P(("groups", "blk")),
        P(),
    )
    return jax.shard_map(
        functools.partial(local, mesh.shape["blk"]),
        mesh=mesh, in_specs=placed, out_specs=P("groups", "blk"), check_vma=False,
    )
```

```python
import functools
import jax
import jax.numpy as jnp
from jax import lax
from jax.experimental import pallas as pl
from jax.experimental.pallas import tpu as pltpu
from jax.sharding import PartitionSpec as P

LANES = 128
DIRECT = 0
NT = (((1,), (1,)), ((), ()))


def make_grads(factors, token_mask):
    rank_size = factors.shape[3] // 2
    mask_values = token_mask.astype(jnp.float32)[:, None, :, None]
    left_side = factors[..., :rank_size].astype(jnp.float32) * mask_values
    right_side = factors[..., rank_size:].astype(jnp.float32)
    outer_sum = jnp.einsum("qlta,qltb->qlab", left_side, right_side)
    return outer_sum.reshape(outer_sum.shape[0], outer_sum.shape[1], rank_size * rank_size).astype(
        jnp.bfloat16
    )


def scale_of(source_ids, source_weight):
    matches = (
        source_ids[:, None] == jnp.arange(source_weight.shape[0], dtype=jnp.int32)[None, :]
    ).astype(jnp.float32)
    return jnp.sum(matches * source_weight[None, :], axis=1)


def plain(factors, token_mask, store, inv_fisher, source_ids, source_weight):
    query_grads = make_grads(factors, token_mask)
    layer_count = inv_fisher.shape[0]
    segment = lax.all_gather(query_grads, "blk", axis=0, tiled=True)
    products = [
        lax.dot_general(
            segment[:, layer_idx], inv_fisher[layer_idx], NT, preferred_element_type=jnp.float32
        )
        for layer_idx in range(layer_count)
    ]
    hidden_cols = jnp.stack(products, axis=1).astype(jnp.bfloat16)
    hidden = lax.all_to_all(hidden_cols, "blk", split_axis=0, concat_axis=2, tiled=True)
    raw_scores = lax.dot_general(
        lax.all_gather(hidden, "blk", axis=0, tiled=True),
        store,
        (((1, 2), (1, 2)), ((), ())),
        preferred_element_type=jnp.float32,
    )
    return raw_scores * scale_of(source_ids, source_weight)[None, :]


class Gather:
    def __init__(self, buf, send_sems, recv_sems, sizes):
        self.buf, self.send_sems, self.recv_sems = buf, send_sems, recv_sems
        self.outer, self.ys, self.cores = sizes
        me = lax.axis_index("blk")
        self.me = me
        self.c = lax.rem(me, self.cores)
        self.y = lax.rem(me // self.cores, self.ys)
        self.z = me // (self.cores * self.ys)
        zs, ys, cs = (range(1, size) for size in sizes)
        self.z_peers = [self.index(k, 0, 0) for k in zs]
        self.y_peers = [self.index(0, j, 0) for j in ys]
        self.c_peers = [self.index(0, 0, i) for i in cs]
        self.across = [self.index(0, j, i) for j in ys for i in cs]
        self.slots = {
            (k, j, i): self.index(k, j, i)
            for k in range(self.outer)
            for j in range(self.ys)
            for i in range(self.cores)
        }

    def index(self, dz, dy, dc):
        if self.outer & (self.outer - 1):
            z = lax.rem(self.z + dz, self.outer)
        else:
            z, bit = self.z, 1
            while bit <= dz:
                if dz & bit:
                    z = z + bit - 2 * bit * lax.rem(z // bit, 2)
                bit *= 2
        y = lax.rem(self.y + dy, self.ys)
        c = lax.rem(self.c + dc, self.cores)
        return (z * self.ys + y) * self.cores + c

    def peers(self):
        across = self.across if DIRECT else []
        return self.z_peers + self.y_peers + self.c_peers + across

    def direct(self, k):
        return k >= self.outer - DIRECT

    def copy(self, slot, l, target):
        block = self.buf.at[slot, l]
        return pltpu.make_async_remote_copy(
            src_ref=block,
            dst_ref=block,
            send_sem=self.send_sems.at[l],
            recv_sem=self.recv_sems.at[l, slot],
            device_id={"blk": target},
            device_id_type=pl.DeviceIdType.MESH,
        )

    def plane(self, k, slot, l):
        for target in self.y_peers + (self.across if self.direct(k) else []) + self.c_peers:
            self.copy(slot, l, target).start()

    def start(self, l):
        for target in self.z_peers[::-1]:
            self.copy(self.me, l, target).start()
        self.plane(0, self.me, l)

    def arrive(self, slot, l):
        self.copy(slot, l, self.me).wait_recv()

    def take_z(self, k, l):
        slot = self.slots[k, 0, 0]
        self.arrive(slot, l)
        self.plane(k, slot, l)

    def take_y(self, k, j, l):
        slot = self.slots[k, j, 0]
        self.arrive(slot, l)
        if not self.direct(k):
            for target in self.c_peers:
                self.copy(slot, l, target).start()

    def finish(self):
        for l in range(self.buf.shape[1]):
            sent = self.buf.at[: self.buf.shape[0] - 1, l]
            pltpu.make_async_copy(sent, sent, self.send_sems.at[l]).wait()


def kernel(
    sizes, mask_hbm, factors_hbm, ids_hbm, weight_hbm, fisher_hbm, store_hbm, out_ref,
    mask_ref, factors_ref, ids_ref, weight_ref,
    fisher, store, grads, hidden, spread, total, turned,
    send_sems, recv_sems, input_sems, fisher_sem, store_sem,
):
    nq, layers, _, width = factors_ref.shape
    rank = width // 2
    rows = rank * rank // LANES
    n = grads.shape[0]
    m = n * nq
    cols = store.shape[2]
    train = out_ref.shape[1]

    first = Gather(grads, send_sems.at[0], recv_sems.at[0], sizes)
    second = Gather(hidden, send_sems.at[1], recv_sems.at[1], sizes)
    me = first.me
    barrier = pltpu.get_barrier_semaphore()
    peers = first.peers()
    for peer in peers:
        pl.semaphore_signal(
            barrier, inc=1, device_id={"blk": peer}, device_id_type=pl.DeviceIdType.MESH
        )
    inputs = [
        pltpu.make_async_copy(source, target, input_sems.at[i])
        for i, (source, target) in enumerate(
            (
                (factors_hbm, factors_ref),
                (mask_hbm, mask_ref),
                (ids_hbm, ids_ref),
                (weight_hbm, weight_ref),
            )
        )
    ]
    for one in inputs:
        one.start()
    for one in inputs[:2]:
        one.wait()

    row = lax.broadcasted_iota(jnp.int32, (rows, width), 0)
    lane = lax.broadcasted_iota(jnp.int32, (rows, width), 1)
    picks = [(lane == 2 * row + par).astype(jnp.bfloat16) for par in range(2)]
    for l in range(layers):
        for q in range(nq):
            block = factors_ref[q, l]
            wide = block.astype(jnp.float32)
            high = lax.broadcasted_iota(jnp.int32, wide.shape, 1) >= rank
            rights = [
                jnp.where(high, 0.0, pltpu.roll(wide, rank, 1)).astype(jnp.bfloat16),
                jnp.where(high, wide, 0.0).astype(jnp.bfloat16),
            ]
            keep = mask_ref[q : q + 1, :].astype(jnp.float32)
            grad = None
            for par in range(2):
                left = lax.dot_general(picks[par], block, NT, preferred_element_type=jnp.float32)
                left = (left * keep).astype(jnp.bfloat16)
                term = jnp.dot(left, rights[par], preferred_element_type=jnp.float32)
                grad = term if grad is None else grad + term
            grads[me, l, q * rows : (q + 1) * rows, :] = grad.astype(jnp.bfloat16)
        if l == 0:
            pl.semaphore_wait(barrier, len(peers))
        first.start(l)

    pltpu.make_async_copy(fisher_hbm, fisher, fisher_sem).start()
    pairs = store_hbm.reshape(train * layers, store_hbm.shape[2])
    for slot in range(n):
        pltpu.make_async_copy(
            pairs.at[:, slot * cols : (slot + 1) * cols], store.at[slot], store_sem
        ).start()
    for one in inputs[2:]:
        one.wait()
    ids = ids_ref[...]
    scale = jnp.zeros(ids.shape, jnp.float32)
    for source in range(weight_ref.shape[0]):
        scale = scale + jnp.where(ids == source, weight_ref[source], 0.0)

    def place(slot, l):
        for q in range(nq):
            spread[l, pl.ds(slot * nq + q, rows, stride=m), :] = grads[
                slot, l, q * rows : (q + 1) * rows, :
            ].astype(jnp.float32)

    def precondition(l):
        left = jnp.concatenate(
            [spread[l, r * m : (r + 1) * m, :].astype(jnp.bfloat16) for r in range(rows)], axis=1
        )
        if l == 0:
            pltpu.make_async_copy(fisher_hbm, fisher, fisher_sem).wait()
        half = fisher.shape[2] // 2
        product = lax.dot_general(
            left[:, :half], fisher[l, :, :half], NT, preferred_element_type=jnp.float32
        ) + lax.dot_general(
            left[:, half:], fisher[l, :, half:], NT, preferred_element_type=jnp.float32
        )
        hidden[me, l] = product.astype(jnp.bfloat16)
        second.start(l)

    for l in range(layers):
        place(me, l)
    outer, ys, cores = sizes
    flat = [(k, j) for k in range(outer) for j in range(1, ys)]
    ends = [(k, j, i) for j in range(ys) for k in range(outer) for i in range(1, cores)]
    for l in range(layers):
        for k in range(1, outer):
            first.take_z(k, l)
            place(first.slots[k, 0, 0], l)
    for l in range(layers):
        for k, j in flat:
            first.take_y(k, j, l)
            place(first.slots[k, j, 0], l)
    for l in range(layers):
        for at in ends:
            first.arrive(first.slots[at], l)
            place(first.slots[at], l)
        precondition(l)

    pltpu.make_async_copy(store, store, store_sem).wait()

    def add(slot, fresh=False):
        left = jnp.concatenate([hidden[slot, l] for l in range(layers)], axis=0)
        term = lax.dot_general(left, store[slot], NT, preferred_element_type=jnp.float32)
        total[...] = term if fresh else total[...] + term

    add(me, True)
    for l in range(layers):
        for k in range(1, outer):
            second.take_z(k, l)
            if l == layers - 1:
                add(second.slots[k, 0, 0])
    early = ends[: outer * (cores - 1)]
    for at in range(max(len(flat), len(early))):
        for k, j in flat[at : at + 1]:
            for l in range(layers):
                second.take_y(k, j, l)
            add(second.slots[k, j, 0])
        for where in early[at : at + 1]:
            for l in range(layers):
                second.arrive(second.slots[where], l)
            add(second.slots[where])
    for where in ends[len(early) :]:
        for l in range(layers):
            second.arrive(second.slots[where], l)
        add(second.slots[where])

    turned[:, : layers * m] = total[...].T
    answer = None
    for l in range(layers):
        part = turned[pl.ds(l, train, stride=layers), :][:, l * m : (l + 1) * m]
        answer = part if answer is None else answer + part
    out_ref[...] = answer.T * scale
    first.finish()
    second.finish()


def fused(n, factors, token_mask, store, inv_fisher, source_ids, source_weight):
    nq, layers, _, width = factors.shape
    train, _, feat = store.shape
    cols = inv_fisher.shape[1]
    m = n * nq
    rows = feat // LANES
    cores = 2 if n % 2 == 0 else 1
    ys = 2 if n % 4 == 0 else 1
    sizes = (n // (cores * ys), ys, cores)
    anyspace = pl.BlockSpec(memory_space=pl.ANY)
    return pl.pallas_call(
        functools.partial(kernel, sizes),
        out_shape=pltpu.VMEM((m, train), jnp.float32),
        in_specs=[anyspace] * 6,
        out_specs=pl.BlockSpec(memory_space=pltpu.VMEM),
        scratch_shapes=[
            pltpu.VMEM(token_mask.shape, token_mask.dtype),
            pltpu.VMEM(factors.shape, factors.dtype),
            pltpu.VMEM((1, train), source_ids.dtype),
            pltpu.SMEM(source_weight.shape, source_weight.dtype),
            pltpu.VMEM((layers, cols, feat), jnp.bfloat16),
            pltpu.VMEM((n, train * layers, cols), jnp.bfloat16),
            pltpu.VMEM((n, layers, nq * rows, LANES), jnp.bfloat16),
            pltpu.VMEM((n, layers, m, cols), jnp.bfloat16),
            pltpu.VMEM((layers, rows * m, LANES), jnp.float32),
            pltpu.VMEM((layers * m, train * layers), jnp.float32),
            pltpu.VMEM((train * layers, LANES), jnp.float32),
            pltpu.SemaphoreType.DMA((2, layers)),
            pltpu.SemaphoreType.DMA((2, layers, n)),
            pltpu.SemaphoreType.DMA((4,)),
            pltpu.SemaphoreType.DMA(()),
            pltpu.SemaphoreType.DMA(()),
        ],
        compiler_params=pltpu.CompilerParams(
            collective_id=0, has_side_effects=True, vmem_limit_bytes=60 * 2**20
        ),
        name="scores",
    )(token_mask, factors, source_ids[None, :], source_weight, inv_fisher, store)


def local(n, factors, token_mask, store, inv_fisher, source_ids, source_weight):
    nq, layers, _, width = factors.shape
    train, _, feat = store.shape
    cols = inv_fisher.shape[1]
    m = n * nq
    held = 2 * (inv_fisher.size + store.size) + 4 * layers * m * train * layers
    fits = (
        width == LANES
        and feat * 4 == width * width
        and cols % LANES == 0
        and layers == 2
        and m % 16 == 0
        and layers * m <= LANES
        and train % LANES == 0
        and held < 40 * 2**20
    )
    if not fits:
        return plain(factors, token_mask, store, inv_fisher, source_ids, source_weight)
    return fused(n, factors, token_mask, store, inv_fisher, source_ids, source_weight)


def solution(mesh):
    placed = (
        P(("groups", "blk"), None, None, None),
        P(("groups", "blk"), None),
        P(("groups", "blk"), None, None),
        P(None, "blk", None),
        P(("groups", "blk")),
        P(),
    )
    return jax.shard_map(
        functools.partial(local, mesh.shape["blk"]),
        mesh=mesh, in_specs=placed, out_specs=P("groups", "blk"), check_vma=False,
    )
```

```python
import functools
import jax
import jax.numpy as jnp
from jax import lax
from jax.experimental import pallas as pl
from jax.experimental.pallas import tpu as pltpu
from jax.sharding import PartitionSpec as P

LANES = 128
NT = (((1,), (1,)), ((), ()))


def make_grads(factors, token_mask):
    rank_size = factors.shape[3] // 2
    mask_values = token_mask.astype(jnp.float32)[:, None, :, None]
    left_side = factors[..., :rank_size].astype(jnp.float32) * mask_values
    right_side = factors[..., rank_size:].astype(jnp.float32)
    outer_sum = jnp.einsum("qlta,qltb->qlab", left_side, right_side)
    return outer_sum.reshape(outer_sum.shape[0], outer_sum.shape[1], rank_size * rank_size).astype(
        jnp.bfloat16
    )


def scale_of(source_ids, source_weight):
    matches = (
        source_ids[:, None] == jnp.arange(source_weight.shape[0], dtype=jnp.int32)[None, :]
    ).astype(jnp.float32)
    return jnp.sum(matches * source_weight[None, :], axis=1)


def plain(factors, token_mask, store, inv_fisher, source_ids, source_weight):
    query_grads = make_grads(factors, token_mask)
    layer_count = inv_fisher.shape[0]
    segment = lax.all_gather(query_grads, "blk", axis=0, tiled=True)
    products = [
        lax.dot_general(
            segment[:, layer_idx], inv_fisher[layer_idx], NT, preferred_element_type=jnp.float32
        )
        for layer_idx in range(layer_count)
    ]
    hidden_cols = jnp.stack(products, axis=1).astype(jnp.bfloat16)
    hidden = lax.all_to_all(hidden_cols, "blk", split_axis=0, concat_axis=2, tiled=True)
    raw_scores = lax.dot_general(
        lax.all_gather(hidden, "blk", axis=0, tiled=True),
        store,
        (((1, 2), (1, 2)), ((), ())),
        preferred_element_type=jnp.float32,
    )
    return raw_scores * scale_of(source_ids, source_weight)[None, :]


class Gather:
    def __init__(self, buf, send_sems, recv_sems, sizes):
        self.buf, self.send_sems, self.recv_sems = buf, send_sems, recv_sems
        self.outer, self.ys, self.cores = sizes
        me = lax.axis_index("blk")
        self.me = me
        self.c = lax.rem(me, self.cores)
        self.y = lax.rem(me // self.cores, self.ys)
        self.z = me // (self.cores * self.ys)
        zs, ys, cs = (range(1, size) for size in sizes)
        self.z_peers = [self.index(k, 0, 0) for k in zs]
        self.y_peers = [self.index(0, j, 0) for j in ys]
        self.c_peers = [self.index(0, 0, i) for i in cs]
        self.far_first = self.z_peers[::-1]
        if self.outer == 4:
            inner = lax.rem(self.z + self.z // 2, 2) == 1
            near, b, c = self.z_peers
            self.far_first = [jnp.where(inner, b, c), jnp.where(inner, c, b), near]
        self.slots = {
            (k, j, i): self.index(k, j, i)
            for k in range(self.outer)
            for j in range(self.ys)
            for i in range(self.cores)
        }

    def index(self, dz, dy, dc):
        if self.outer & (self.outer - 1):
            z = lax.rem(self.z + dz, self.outer)
        else:
            z, bit = self.z, 1
            while bit <= dz:
                if dz & bit:
                    z = z + bit - 2 * bit * lax.rem(z // bit, 2)
                bit *= 2
        y = lax.rem(self.y + dy, self.ys)
        c = lax.rem(self.c + dc, self.cores)
        return (z * self.ys + y) * self.cores + c

    def peers(self):
        return self.z_peers + self.y_peers + self.c_peers

    def copy(self, slot, l, target):
        block = self.buf.at[slot, l]
        return pltpu.make_async_remote_copy(
            src_ref=block,
            dst_ref=block,
            send_sem=self.send_sems.at[l],
            recv_sem=self.recv_sems.at[l, slot],
            device_id={"blk": target},
            device_id_type=pl.DeviceIdType.MESH,
        )

    def plane(self, slot, l):
        for target in self.y_peers + self.c_peers:
            self.copy(slot, l, target).start()

    def start(self, l):
        for target in self.far_first:
            self.copy(self.me, l, target).start()
        self.plane(self.me, l)

    def arrive(self, slot, l):
        self.copy(slot, l, self.me).wait_recv()

    def take_z(self, k, l):
        slot = self.slots[k, 0, 0]
        self.arrive(slot, l)
        self.plane(slot, l)

    def take_y(self, k, j, l):
        slot = self.slots[k, j, 0]
        self.arrive(slot, l)
        for target in self.c_peers:
            self.copy(slot, l, target).start()

    def finish(self):
        for l in range(self.buf.shape[1]):
            sent = self.buf.at[: self.buf.shape[0] - 1, l]
            pltpu.make_async_copy(sent, sent, self.send_sems.at[l]).wait()


def kernel(
    sizes, mask_hbm, factors_hbm, ids_hbm, weight_hbm, fisher_hbm, store_hbm, out_ref,
    mask_ref, factors_ref, ids_ref, weight_ref,
    fisher, store, grads, hidden, spread, total, turned,
    send_sems, recv_sems, input_sems, fisher_sem, store_sem,
):
    nq, layers, _, width = factors_ref.shape
    rank = width // 2
    rows = rank * rank // LANES
    n = grads.shape[0]
    m = n * nq
    cols = store.shape[2]
    train = out_ref.shape[1]

    first = Gather(grads, send_sems.at[0], recv_sems.at[0], sizes)
    second = Gather(hidden, send_sems.at[1], recv_sems.at[1], sizes)
    me = first.me
    barrier = pltpu.get_barrier_semaphore()
    peers = first.peers()
    for peer in peers:
        pl.semaphore_signal(
            barrier, inc=1, device_id={"blk": peer}, device_id_type=pl.DeviceIdType.MESH
        )
    inputs = [
        pltpu.make_async_copy(source, target, input_sems.at[i])
        for i, (source, target) in enumerate(
            (
                (factors_hbm, factors_ref),
                (mask_hbm, mask_ref),
                (ids_hbm, ids_ref),
                (weight_hbm, weight_ref),
            )
        )
    ]
    for one in inputs:
        one.start()
    for one in inputs[:2]:
        one.wait()

    row = lax.broadcasted_iota(jnp.int32, (rows, width), 0)
    lane = lax.broadcasted_iota(jnp.int32, (rows, width), 1)
    picks = [(lane == 2 * row + par).astype(jnp.bfloat16) for par in range(2)]
    for l in range(layers):
        for q in range(nq):
            block = factors_ref[q, l]
            wide = block.astype(jnp.float32)
            high = lax.broadcasted_iota(jnp.int32, wide.shape, 1) >= rank
            rights = [
                jnp.where(high, 0.0, pltpu.roll(wide, rank, 1)).astype(jnp.bfloat16),
                jnp.where(high, wide, 0.0).astype(jnp.bfloat16),
            ]
            keep = mask_ref[q : q + 1, :].astype(jnp.float32)
            grad = None
            for par in range(2):
                left = lax.dot_general(picks[par], block, NT, preferred_element_type=jnp.float32)
                left = (left * keep).astype(jnp.bfloat16)
                term = jnp.dot(left, rights[par], preferred_element_type=jnp.float32)
                grad = term if grad is None else grad + term
            grads[me, l, q * rows : (q + 1) * rows, :] = grad.astype(jnp.bfloat16)
        if l == 0:
            pl.semaphore_wait(barrier, len(peers))
        first.start(l)

    for one in inputs[2:]:
        one.wait()
    ids = ids_ref[...]
    scale = jnp.zeros(ids.shape, jnp.float32)
    for source in range(weight_ref.shape[0]):
        scale = scale + jnp.where(ids == source, weight_ref[source], 0.0)

    def place(slot, l):
        for q in range(nq):
            spread[l, pl.ds(slot * nq + q, rows, stride=m), :] = grads[
                slot, l, q * rows : (q + 1) * rows, :
            ].astype(jnp.float32)

    def precondition(l):
        left = jnp.concatenate(
            [spread[l, r * m : (r + 1) * m, :].astype(jnp.bfloat16) for r in range(rows)], axis=1
        )
        if l == 0:
            pltpu.make_async_copy(fisher_hbm, fisher, fisher_sem).wait()
        for at in range(0, cols, LANES):
            product = lax.dot_general(
                left, fisher[l, at : at + LANES], NT, preferred_element_type=jnp.float32
            )
            hidden[me, l, :, at : at + LANES] = product.astype(jnp.bfloat16)
        second.start(l)

    pltpu.make_async_copy(fisher_hbm, fisher, fisher_sem).start()
    pairs = store_hbm.reshape(train * layers, store_hbm.shape[2])
    for slot in range(n):
        pltpu.make_async_copy(
            pairs.at[:, slot * cols : (slot + 1) * cols], store.at[slot], store_sem
        ).start()
    for l in range(layers):
        place(me, l)
    outer, ys, cores = sizes
    flat = [(k, j) for k in range(outer) for j in range(1, ys)]
    ends = [(k, j, i) for j in range(ys) for k in range(outer) for i in range(1, cores)]
    for l in range(layers):
        for k in range(1, outer):
            first.take_z(k, l)
            place(first.slots[k, 0, 0], l)
    for l in range(layers):
        for k, j in flat:
            first.take_y(k, j, l)
            place(first.slots[k, j, 0], l)
    for l in range(layers):
        for at in ends:
            first.arrive(first.slots[at], l)
            place(first.slots[at], l)
        precondition(l)

    pltpu.make_async_copy(store, store, store_sem).wait()

    def add(slot, fresh=False):
        left = jnp.concatenate([hidden[slot, l] for l in range(layers)], axis=0)
        term = lax.dot_general(left, store[slot], NT, preferred_element_type=jnp.float32)
        total[...] = term if fresh else total[...] + term

    add(me, True)
    for l in range(layers):
        for k in range(1, outer):
            second.take_z(k, l)
            if l == layers - 1:
                add(second.slots[k, 0, 0])
    early = ends[: outer * (cores - 1)]
    for at in range(max(len(flat), len(early))):
        for k, j in flat[at : at + 1]:
            for l in range(layers):
                second.take_y(k, j, l)
            add(second.slots[k, j, 0])
        for where in early[at : at + 1]:
            for l in range(layers):
                second.arrive(second.slots[where], l)
            add(second.slots[where])
    for where in ends[len(early) :]:
        for l in range(layers):
            second.arrive(second.slots[where], l)
        add(second.slots[where])

    scores = total[...]
    layer = lax.rem(lax.broadcasted_iota(jnp.int32, (m, scores.shape[1]), 1), layers)
    own = scores[:m]
    for l in range(1, layers):
        own = jnp.where(layer == l, scores[l * m : (l + 1) * m], own)
    turned[:, :m] = own.T
    answer = None
    for l in range(layers):
        part = turned[pl.ds(l, train, stride=layers), :][:, :m]
        answer = part if answer is None else answer + part
    out_ref[...] = answer.T * scale
    first.finish()
    second.finish()


def fused(n, factors, token_mask, store, inv_fisher, source_ids, source_weight):
    nq, layers, _, width = factors.shape
    train, _, feat = store.shape
    cols = inv_fisher.shape[1]
    m = n * nq
    rows = feat // LANES
    cores = 2 if n % 2 == 0 else 1
    ys = 2 if n % 4 == 0 else 1
    sizes = (n // (cores * ys), ys, cores)
    anyspace = pl.BlockSpec(memory_space=pl.ANY)
    return pl.pallas_call(
        functools.partial(kernel, sizes),
        out_shape=pltpu.VMEM((m, train), jnp.float32),
        in_specs=[anyspace] * 6,
        out_specs=pl.BlockSpec(memory_space=pltpu.VMEM),
        scratch_shapes=[
            pltpu.VMEM(token_mask.shape, token_mask.dtype),
            pltpu.VMEM(factors.shape, factors.dtype),
            pltpu.VMEM((1, train), source_ids.dtype),
            pltpu.SMEM(source_weight.shape, source_weight.dtype),
            pltpu.VMEM((layers, cols, feat), jnp.bfloat16),
            pltpu.VMEM((n, train * layers, cols), jnp.bfloat16),
            pltpu.VMEM((n, layers, nq * rows, LANES), jnp.bfloat16),
            pltpu.VMEM((n, layers, m, cols), jnp.bfloat16),
            pltpu.VMEM((layers, rows * m, LANES), jnp.float32),
            pltpu.VMEM((layers * m, train * layers), jnp.float32),
            pltpu.VMEM((train * layers, LANES), jnp.float32),
            pltpu.SemaphoreType.DMA((2, layers)),
            pltpu.SemaphoreType.DMA((2, layers, n)),
            pltpu.SemaphoreType.DMA((4,)),
            pltpu.SemaphoreType.DMA(()),
            pltpu.SemaphoreType.DMA(()),
        ],
        compiler_params=pltpu.CompilerParams(
            collective_id=0, has_side_effects=True, vmem_limit_bytes=60 * 2**20
        ),
        name="scores",
    )(token_mask, factors, source_ids[None, :], source_weight, inv_fisher, store)


def local(n, factors, token_mask, store, inv_fisher, source_ids, source_weight):
    nq, layers, _, width = factors.shape
    train, _, feat = store.shape
    cols = inv_fisher.shape[1]
    m = n * nq
    held = 2 * (inv_fisher.size + store.size) + 4 * layers * m * train * layers
    fits = (
        width == LANES
        and feat * 4 == width * width
        and cols % LANES == 0
        and layers == 2
        and m % 16 == 0
        and layers * m <= LANES
        and train % LANES == 0
        and held < 40 * 2**20
    )
    if not fits:
        return plain(factors, token_mask, store, inv_fisher, source_ids, source_weight)
    return fused(n, factors, token_mask, store, inv_fisher, source_ids, source_weight)


def solution(mesh):
    placed = (
        P(("groups", "blk"), None, None, None),
        P(("groups", "blk"), None),
        P(("groups", "blk"), None, None),
        P(None, "blk", None),
        P(("groups", "blk")),
        P(),
    )
    return jax.shard_map(
        functools.partial(local, mesh.shape["blk"]),
        mesh=mesh, in_specs=placed, out_specs=P("groups", "blk"), check_vma=False,
    )
```
